512 devices in a mesh: freq: 16 (over z_lo, x), tm: 32 (over z_hi, y, core).
Axes of the slice: x: 4, y: 8, z: 8 (z_hi: 2, z_lo: 4; z = z_hi * 4 + z_lo), core: 2. Of those that a mesh axis runs over, the one named last changes fastest.
Arguments:
- baseband: bfloat16 [128, 4, 262144], P('freq', None, 'tm'), may hold values from -3 to 3
- chirp_phase: float32 [128, 16384], P('freq'), may hold values from -3.140625 to 3.140625
- phase_bins: int32 [262144], P('tm'), may hold values from 0 to 1023
Outputs:
- profile: float32 [128, 4, 1024], P('freq', None, 'tm')
The draws below stay inside these ranges and needn't reach their ends.
Inputs may be any that keep to these rules, and one draw needn't show every extreme that they name: `phase_bins`: each time sample's phase bin.
All inputs are finite; a program needn't handle non-finite values.
Results may differ from the reference program's by a relative error of at most 0.0003.
Values may be sent and summed in bfloat16 or wider, within the bound.
A program may use at most 64 MiB of HBM per device.

```python
import jax
import jax.numpy as jnp
from jax import lax

BINS = 1024
NFFT = 16384
NOVL = 8192
CHANNELS = 128
TIME = 262144


def touch_ends(entries, own_key, low, top_value):
    place = [jax.random.randint(jax.random.fold_in(own_key, axis), (), 0, length) for axis, length in enumerate(entries.shape)]
    longest = entries.shape.index(max(entries.shape))
    neighbour = place[:longest] + [(place[longest] + 1) % entries.shape[longest]] + place[longest + 1:]
    return entries.at[tuple(place)].set(low).at[tuple(neighbour)].set(top_value)


def block_scale(own_key, dims, pieces, smallest, top_value):
    gain, own = 1.0, jax.random.fold_in(own_key, 6)
    for dim, blocks in pieces:
        steps = jnp.exp(jax.random.uniform(jax.random.fold_in(own, dim), (blocks,), jnp.float32, smallest / len(pieces), top_value / len(pieces)))
        gain = gain * jnp.repeat(steps, dims[dim] // blocks).reshape([-1 if axis == dim else 1 for axis in range(len(dims))])
    return gain


def normal_values(key, extent, spread, limit, shards=(), kind=jnp.bfloat16):
    array = jax.random.normal(key, extent, jnp.float32) * spread
    if len(shards) > 0:
        array = block_scale(key, extent, shards, -0.22, 0.18) * array
    return jnp.clip(array, min=-limit, max=limit).astype(kind)


def setup_inputs(seed: int = 0) -> dict:
    splits = jax.random.split(jax.random.key(seed), 4)
    baseband = normal_values(splits[0], (CHANNELS, 4, TIME), 0.5, 3.0, ((0, 16), (2, 32)))
    chirp_phase = jnp.clip(jax.random.uniform(splits[1], (CHANNELS, NFFT), jnp.float32, -3.140625, 3.140625), -3.140625, 3.140625)
    phase_bins = touch_ends(jax.random.randint(splits[2], (TIME,), 0, BINS), jax.random.fold_in(splits[2], 1), 0, BINS - 1).astype(jnp.int32)
    return dict(baseband=baseband, chirp_phase=chirp_phase, phase_bins=phase_bins)


def reference(baseband, chirp_phase, phase_bins):
    samples_all = baseband.shape[2]
    frame_count = samples_all // NOVL

    def one_channel(channel_item):
        samples, phases = channel_item
        samples = samples.astype(jnp.float32)
        response = jnp.cos(phases) + 1j * jnp.sin(phases)
        filtered = []
        for polar in range(2):
            series = samples[2 * polar] + 1j * samples[2 * polar + 1]
            padded = jnp.concatenate([jnp.zeros((NOVL,), series.dtype), series])
            blocks = padded.reshape(frame_count + 1, NOVL)
            frames = jnp.concatenate([blocks[:-1], blocks[1:]], axis=1)
            spectra = jnp.fft.fft(frames, axis=1) * response[None, :]
            waves = jnp.fft.ifft(spectra, axis=1)[:, NOVL:]
            filtered.append(waves.reshape(samples_all))
        first_real = jnp.real(filtered[0])
        first_imag = jnp.imag(filtered[0])
        second_real = jnp.real(filtered[1])
        second_imag = jnp.imag(filtered[1])
        power_first = first_real * first_real + first_imag * first_imag
        power_second = second_real * second_real + second_imag * second_imag
        stokes = jnp.stack([
            power_first + power_second,
            power_first - power_second,
            2.0 * (first_real * second_real + first_imag * second_imag),
            2.0 * (first_real * second_imag - first_imag * second_real),
        ])
        folded = jax.ops.segment_sum(stokes.T, phase_bins, num_segments=BINS)
        return folded.T

    profile = lax.map(one_channel, (baseband, chirp_phase))
    return profile / float(samples_all // BINS)
```

```python
import functools

import jax
import jax.numpy as jnp
import numpy as np
from jax import lax
from jax.experimental import pallas as pl
from jax.experimental.pallas import tpu as pltpu
from jax.sharding import PartitionSpec as P

BINS = 1024
RADIX = 128
HALF = 64
LOW_BINS = 256
F32 = jnp.float32
BF16 = jnp.bfloat16


def split_table(table):
    high = table.astype(jnp.bfloat16)
    low = (table - high.astype(np.float64)).astype(jnp.bfloat16)
    return high, low


def dft_tables():
    index = np.arange(RADIX)
    angle = 2.0 * np.pi * (index[:, None] * index[None, :] % RADIX) / RADIX
    four_real, four_imag = np.cos(angle), -np.sin(angle)
    turn = 2.0 * np.pi * (index[:, None] * index[None, :]) / (RADIX * RADIX)
    twist = np.concatenate([np.cos(turn), -np.sin(turn)], axis=1).astype(np.float32)
    left = np.block([[four_real, -four_imag], [four_imag, four_real]])
    right = np.block([[four_real, four_imag], [-four_imag, four_real]])
    back_right = np.block([[four_real, -four_imag], [four_imag, four_real]]) / RADIX
    kept_real, kept_imag = four_real[HALF:], four_imag[HALF:]
    back_left = np.block([[kept_real, kept_imag], [-kept_imag, kept_real]]) / RADIX
    tables = []
    for table in (left, right, back_right, back_left):
        tables.extend(split_table(table))
    return tables, twist


def halves(value):
    high = value.astype(BF16)
    low = (value - high.astype(F32)).astype(BF16)
    return high, low


def dot(a, b):
    return jnp.dot(a, b, preferred_element_type=F32)


def cos_sin(phase):
    half = phase * 0.5
    square = half * half
    sine = half * (
        1.0 + square * (-1.0 / 6 + square * (1.0 / 120 + square * (-1.0 / 5040 + square * (
            1.0 / 362880 + square * (-1.0 / 39916800 + square * (1.0 / 6227020800))))))
    )
    cosine = 1.0 + square * (-1.0 / 2 + square * (1.0 / 24 + square * (-1.0 / 720 + square * (
        1.0 / 40320 + square * (-1.0 / 3628800 + square * (
            1.0 / 479001600 + square * (-1.0 / 87178291200))))))
    )
    return 1.0 - 2.0 * sine * sine, 2.0 * sine * cosine


def work_kernel(
    channels, prev, cur, chirp, bins, left_h, left_l, right_h, right_l, back_right_h,
    back_right_l, back_left_h, back_left_l, twist, out, stokes, picked, onehot,
):
    rows = 4 * channels
    twist_real = twist[:, :RADIX]
    twist_imag = twist[:, RADIX:]
    wide_real = jnp.concatenate([twist_real, twist_real], axis=1)
    wide_imag = jnp.concatenate([twist_imag, twist_imag], axis=1)

    def channel(c, carry):
        base = 4 * c

        def pair(part):
            old = jnp.concatenate([prev[base + part], prev[base + 2 + part]], axis=1)
            new = jnp.concatenate([cur[base + part], cur[base + 2 + part]], axis=1)
            return jnp.concatenate([old, new], axis=0)

        series = jnp.concatenate([pair(0), pair(1)], axis=0)
        section = dot(left_h[...], series) + dot(left_l[...], series)
        real, imag = section[:RADIX], section[RADIX:]
        turned_real = real * wide_real - imag * wide_imag
        turned_imag = real * wide_imag + imag * wide_real
        gain_real, gain_imag = cos_sin(chirp[c].T)
        waves_real, waves_imag = [], []
        for p in range(2):
            lanes = slice(p * RADIX, (p + 1) * RADIX)
            high, low = halves(
                jnp.concatenate([turned_real[:, lanes], turned_imag[:, lanes]], axis=1)
            )
            spec = dot(high, right_h[...]) + dot(low, right_h[...]) + dot(high, right_l[...])
            spec_real, spec_imag = spec[:, :RADIX], spec[:, RADIX:]
            high, low = halves(
                jnp.concatenate(
                    [
                        spec_real * gain_real - spec_imag * gain_imag,
                        spec_real * gain_imag + spec_imag * gain_real,
                    ],
                    axis=1,
                )
            )
            back = (
                dot(high, back_right_h[...])
                + dot(low, back_right_h[...])
                + dot(high, back_right_l[...])
            )
            back_real, back_imag = back[:, :RADIX], back[:, RADIX:]
            waves_real.append(back_real * twist_real + back_imag * twist_imag)
            waves_imag.append(back_imag * twist_real - back_real * twist_imag)
        high, low = halves(
            jnp.concatenate(
                [jnp.concatenate(waves_real, axis=1), jnp.concatenate(waves_imag, axis=1)], axis=0
            )
        )
        wave = (
            dot(back_left_h[...], high) + dot(back_left_h[...], low) + dot(back_left_l[...], high)
        )
        xr, xi = wave[:HALF, :RADIX], wave[HALF:, :RADIX]
        yr, yi = wave[:HALF, RADIX:], wave[HALF:, RADIX:]
        first = xr * xr + xi * xi
        second = yr * yr + yi * yi
        stokes[pl.ds(base, HALF, rows), :] = first + second
        stokes[pl.ds(base + 1, HALF, rows), :] = first - second
        stokes[pl.ds(base + 2, HALF, rows), :] = 2.0 * (xr * yr + xi * yi)
        stokes[pl.ds(base + 3, HALF, rows), :] = 2.0 * (xr * yi - xi * yr)
        return carry

    lax.fori_loop(0, channels, channel, 0)

    groups = BINS // LOW_BINS
    lane_bins = lax.broadcasted_iota(jnp.int32, (LOW_BINS, 2 * RADIX), 0)

    def pick(m, carry):
        start = pl.multiple_of(m * 2 * rows, 2 * rows)
        value = jnp.concatenate(
            [stokes[pl.ds(start, rows), :], stokes[pl.ds(start + rows, rows), :]], axis=1
        )
        high = value.astype(BF16).astype(F32)
        both = jnp.concatenate([high, value - high], axis=0)
        own = bins[pl.ds(m, 1), :]
        group = own // LOW_BINS
        columns = pl.ds(pl.multiple_of(m * 2 * RADIX, 2 * RADIX), 2 * RADIX)
        for q in range(groups):
            picked[pl.ds(q * 2 * rows, 2 * rows), columns] = jnp.where(
                group == q, both, 0.0
            ).astype(BF16)
        onehot[:, columns] = jnp.where(
            lane_bins == own - group * LOW_BINS, 1.0, 0.0
        ).astype(BF16)
        return carry

    lax.fori_loop(0, HALF // 2, pick, 0)

    total = lax.dot_general(
        picked[...], onehot[...], (((1,), (1,)), ((), ())), preferred_element_type=F32
    )
    for q in range(groups):
        at = q * 2 * rows
        folded = total[at:at + rows] + total[at + rows:at + 2 * rows]
        for h in range(2):
            for b in range(4):
                lanes = slice(h * RADIX + 32 * b, h * RADIX + 32 * b + 32)
                out[q * 8 + h * 4 + b] = jnp.concatenate(
                    [folded[8 * a:8 * a + 8, lanes] for a in range(4)], axis=1
                )


def sum_kernel(devices, factor, tiles, out, landed, send_sems, recv_sems):
    me = lax.axis_index("tm")

    barrier = pltpu.get_barrier_semaphore()

    def greet(i, carry):
        pl.semaphore_signal(
            barrier, inc=1, device_id={"tm": lax.rem(me + i, devices)},
            device_id_type=pl.DeviceIdType.MESH,
        )
        return carry

    lax.fori_loop(1, devices, greet, 0)
    pl.semaphore_wait(barrier, devices - 1)

    def copy(i):
        peer = lax.rem(me + i, devices)
        return pltpu.make_async_remote_copy(
            src_ref=tiles.at[peer],
            dst_ref=landed.at[i],
            send_sem=send_sems.at[i],
            recv_sem=recv_sems.at[i],
            device_id={"tm": peer},
            device_id_type=pl.DeviceIdType.MESH,
        )

    def send(i, carry):
        copy(i).start()
        return carry

    lax.fori_loop(1, devices, send, 0)

    def take(i, total):
        copy(i).wait_recv()
        return total + landed[i]

    total = lax.fori_loop(1, devices, take, tiles[me]) * factor
    for a in range(4):
        for k in range(2):
            out[2 * a + k] = total[4 * k:4 * k + 4, 32 * a:32 * a + 32]

    def drain(i, carry):
        copy(i).wait_send()
        return carry

    lax.fori_loop(1, devices, drain, 0)


def shards(baseband, chirp_phase, phase_bins):
    channels, _, samples = baseband.shape
    devices = lax.axis_size("tm")
    rows = 4 * channels
    cur = baseband.reshape(rows, HALF, RADIX)
    prev = lax.ppermute(cur, "tm", [(i, i + 1) for i in range(devices - 1)])
    chirp = chirp_phase.reshape(channels, RADIX, RADIX)
    bins = phase_bins.reshape(samples // (2 * RADIX), 2 * RADIX)
    tables, twist = dft_tables()
    in_vmem = pl.BlockSpec(memory_space=pltpu.VMEM)
    tiles = pl.pallas_call(
        functools.partial(work_kernel, channels),
        out_shape=jax.ShapeDtypeStruct((devices, 8, RADIX), F32),
        in_specs=[in_vmem] * 13,
        out_specs=in_vmem,
        scratch_shapes=[
            pltpu.VMEM((HALF * rows, RADIX), F32),
            pltpu.VMEM((8 * rows, samples), BF16),
            pltpu.VMEM((LOW_BINS, samples), BF16),
        ],
        name="work",
    )(prev, cur, chirp, bins, *tables, twist)
    factor = 1.0 / float(samples * devices // BINS)
    return pl.pallas_call(
        functools.partial(sum_kernel, devices, factor),
        out_shape=jax.ShapeDtypeStruct((channels, 4, BINS // devices), F32),
        in_specs=[in_vmem],
        out_specs=in_vmem,
        scratch_shapes=[
            pltpu.VMEM((devices, 8, RADIX), F32),
            pltpu.SemaphoreType.DMA((devices,)),
            pltpu.SemaphoreType.DMA((devices,)),
        ],
        compiler_params=pltpu.CompilerParams(collective_id=0, has_side_effects=True),
        name="sum",
    )(tiles)


def solution(mesh):
    placed = (P("freq", None, "tm"), P("freq", None), P("tm"))
    return jax.shard_map(
        shards, mesh=mesh, in_specs=placed, out_specs=P("freq", None, "tm"), check_vma=False
    )
```

```python
import functools

import jax
import jax.numpy as jnp
import numpy as np
from jax import lax
from jax.experimental import pallas as pl
from jax.experimental.pallas import tpu as pltpu
from jax.sharding import PartitionSpec as P

BINS = 1024
RADIX = 128
HALF = 64
LOW_BINS = 256
F32 = jnp.float32
BF16 = jnp.bfloat16


def split_table(table):
    high = table.astype(jnp.bfloat16)
    low = (table - high.astype(np.float64)).astype(jnp.bfloat16)
    return high, low


def dft_tables():
    index = np.arange(RADIX)
    angle = 2.0 * np.pi * (index[:, None] * index[None, :] % RADIX) / RADIX
    four_real, four_imag = np.cos(angle), -np.sin(angle)
    turn = 2.0 * np.pi * (index[:, None] * index[None, :]) / (RADIX * RADIX)
    twist = np.concatenate([np.cos(turn), -np.sin(turn)], axis=1).astype(np.float32)
    left = np.block([[four_real, -four_imag], [four_imag, four_real]])
    right = np.block([[four_real, four_imag], [-four_imag, four_real]])
    back_right = np.block([[four_real, -four_imag], [four_imag, four_real]]) / RADIX
    kept_real, kept_imag = four_real[HALF:], four_imag[HALF:]
    back_left = np.block([[kept_real, kept_imag], [-kept_imag, kept_real]]) / RADIX
    tables = []
    for part in range(2):
        columns = np.arange(4 * HALF).reshape(4, HALF)[part::2].reshape(-1)
        tables.append(np.concatenate(split_table(left[:, columns]), axis=1))
    for table in (right, back_right, back_left):
        tables.extend(split_table(table))
    return tables, twist


def halves(value):
    high = value.astype(BF16)
    low = (value - high.astype(F32)).astype(BF16)
    return high, low


def dot(a, b):
    return jnp.dot(a, b, preferred_element_type=F32)


def cos_sin(phase):
    half = phase * 0.5
    square = half * half
    sine = half * (
        1.0 + square * (-1.0 / 6 + square * (1.0 / 120 + square * (-1.0 / 5040 + square * (
            1.0 / 362880 + square * (-1.0 / 39916800 + square * (1.0 / 6227020800))))))
    )
    cosine = 1.0 + square * (-1.0 / 2 + square * (1.0 / 24 + square * (-1.0 / 720 + square * (
        1.0 / 40320 + square * (-1.0 / 3628800 + square * (
            1.0 / 479001600 + square * (-1.0 / 87178291200))))))
    )
    return 1.0 - 2.0 * sine * sine, 2.0 * sine * cosine


def paired(block, base, part):
    return jnp.concatenate([block[base + part], block[base + 2 + part]], axis=1)


def first_stage(table, block, base):
    series = jnp.concatenate([paired(block, base, 0), paired(block, base, 1)], axis=0)
    return dot(table[...], jnp.concatenate([series, series], axis=0))


def prep_kernel(channels, cur, chirp, bins, left, gain, part, onehot):
    lane_bins = lax.broadcasted_iota(jnp.int32, (LOW_BINS, 2 * RADIX), 0)

    def channel(c, carry):
        cosine, sine = cos_sin(chirp[c].T)
        gain[c] = jnp.concatenate([cosine, sine], axis=1)
        part[c] = first_stage(left, cur, 4 * c)
        return carry

    lax.fori_loop(0, channels, channel, 0)

    def mark(m, carry):
        own = bins[pl.ds(m, 1), :]
        columns = pl.ds(pl.multiple_of(m * 2 * RADIX, 2 * RADIX), 2 * RADIX)
        onehot[:, columns] = jnp.where(
            lane_bins == own - own // LOW_BINS * LOW_BINS, 1.0, 0.0
        ).astype(BF16)
        return carry

    lax.fori_loop(0, HALF // 2, mark, 0)


def work_kernel(
    channels, devices, factor, prev, gain, part, onehot, bins, left, right_h, right_l,
    back_right_h, back_right_l, back_left_h, back_left_l, twist, out, stokes, picked, tiles,
    landed, send_sems, recv_sems,
):
    me = lax.axis_index("tm")
    barrier = pltpu.get_barrier_semaphore()

    def greet(i, carry):
        pl.semaphore_signal(
            barrier, inc=1, device_id={"tm": lax.rem(me + i, devices)},
            device_id_type=pl.DeviceIdType.MESH,
        )
        return carry

    lax.fori_loop(1, devices, greet, 0)

    rows = 4 * channels
    twist_real = twist[:, :RADIX]
    twist_imag = twist[:, RADIX:]
    wide_real = jnp.concatenate([twist_real, twist_real], axis=1)
    wide_imag = jnp.concatenate([twist_imag, twist_imag], axis=1)

    def channel(c):
        base = 4 * c
        section = part[c] + first_stage(left, prev, base)
        real, imag = section[:RADIX], section[RADIX:]
        turned_real = real * wide_real - imag * wide_imag
        turned_imag = real * wide_imag + imag * wide_real
        gain_real, gain_imag = gain[c, :, :RADIX], gain[c, :, RADIX:]
        waves_real, waves_imag = [], []
        for p in range(2):
            lanes = slice(p * RADIX, (p + 1) * RADIX)
            high, low = halves(
                jnp.concatenate([turned_real[:, lanes], turned_imag[:, lanes]], axis=1)
            )
            spec = dot(high, right_h[...]) + dot(low, right_h[...]) + dot(high, right_l[...])
            spec_real, spec_imag = spec[:, :RADIX], spec[:, RADIX:]
            high, low = halves(
                jnp.concatenate(
                    [
                        spec_real * gain_real - spec_imag * gain_imag,
                        spec_real * gain_imag + spec_imag * gain_real,
                    ],
                    axis=1,
                )
            )
            back = (
                dot(high, back_right_h[...])
                + dot(low, back_right_h[...])
                + dot(high, back_right_l[...])
            )
            back_real, back_imag = back[:, :RADIX], back[:, RADIX:]
            waves_real.append(back_real * twist_real + back_imag * twist_imag)
            waves_imag.append(back_imag * twist_real - back_real * twist_imag)
        high, low = halves(
            jnp.concatenate(
                [jnp.concatenate(waves_real, axis=1), jnp.concatenate(waves_imag, axis=1)], axis=0
            )
        )
        wave = (
            dot(back_left_h[...], high) + dot(back_left_h[...], low) + dot(back_left_l[...], high)
        )
        xr, xi = wave[:HALF, :RADIX], wave[HALF:, :RADIX]
        yr, yi = wave[:HALF, RADIX:], wave[HALF:, RADIX:]
        first = xr * xr + xi * xi
        second = yr * yr + yi * yi
        stokes[pl.ds(base, HALF, rows), :] = first + second
        stokes[pl.ds(base + 1, HALF, rows), :] = first - second
        stokes[pl.ds(base + 2, HALF, rows), :] = 2.0 * (xr * yr + xi * yi)
        stokes[pl.ds(base + 3, HALF, rows), :] = 2.0 * (xr * yi - xi * yr)

    def channel_pair(i, carry):
        channel(2 * i)
        channel(2 * i + 1)
        return carry

    lax.fori_loop(0, channels // 2, channel_pair, 0)

    groups = BINS // LOW_BINS

    def pick(m, carry):
        start = pl.multiple_of(m * 2 * rows, 2 * rows)
        value = jnp.concatenate(
            [stokes[pl.ds(start, rows), :], stokes[pl.ds(start + rows, rows), :]], axis=1
        )
        high = value.astype(BF16).astype(F32)
        both = jnp.concatenate([high, value - high], axis=0)
        group = bins[pl.ds(m, 1), :] // LOW_BINS
        columns = pl.ds(pl.multiple_of(m * 2 * RADIX, 2 * RADIX), 2 * RADIX)
        for q in range(groups):
            picked[pl.ds(q * 2 * rows, 2 * rows), columns] = jnp.where(
                group == q, both, 0.0
            ).astype(BF16)
        return carry

    lax.fori_loop(0, HALF // 2, pick, 0)

    total = lax.dot_general(
        picked[...], onehot[...], (((1,), (1,)), ((), ())), preferred_element_type=F32
    )
    for q in range(groups):
        at = q * 2 * rows
        folded = total[at:at + rows] + total[at + rows:at + 2 * rows]
        for h in range(2):
            for b in range(4):
                lanes = slice(h * RADIX + 32 * b, h * RADIX + 32 * b + 32)
                tiles[q * 8 + h * 4 + b] = jnp.concatenate(
                    [folded[8 * a:8 * a + 8, lanes] for a in range(4)], axis=1
                )

    pl.semaphore_wait(barrier, devices - 1)

    def copy(i):
        peer = lax.rem(me + i, devices)
        return pltpu.make_async_remote_copy(
            src_ref=tiles.at[peer],
            dst_ref=landed.at[i],
            send_sem=send_sems.at[i],
            recv_sem=recv_sems.at[i],
            device_id={"tm": peer},
            device_id_type=pl.DeviceIdType.MESH,
        )

    def send(i, carry):
        copy(i).start()
        return carry

    lax.fori_loop(1, devices, send, 0)

    def take(i, total):
        copy(i).wait_recv()
        return total + landed[i]

    total = lax.fori_loop(1, devices, take, tiles[me]) * factor
    for a in range(4):
        for k in range(2):
            out[2 * a + k] = total[4 * k:4 * k + 4, 32 * a:32 * a + 32]

    def drain(i, carry):
        copy(i).wait_send()
        return carry

    lax.fori_loop(1, devices, drain, 0)


def shards(baseband, chirp_phase, phase_bins):
    channels, _, samples = baseband.shape
    devices = lax.axis_size("tm")
    rows = 4 * channels
    cur = baseband.reshape(rows, HALF, RADIX)
    prev = lax.ppermute(cur, "tm", [(i, i + 1) for i in range(devices - 1)])
    chirp = chirp_phase.reshape(channels, RADIX, RADIX)
    bins = phase_bins.reshape(samples // (2 * RADIX), 2 * RADIX)
    tables, twist = dft_tables()
    in_vmem = pl.BlockSpec(memory_space=pltpu.VMEM)
    gain, part, onehot = pl.pallas_call(
        functools.partial(prep_kernel, channels),
        out_shape=[
            jax.ShapeDtypeStruct((channels, RADIX, 2 * RADIX), F32),
            jax.ShapeDtypeStruct((channels, 2 * RADIX, 2 * RADIX), F32),
            jax.ShapeDtypeStruct((LOW_BINS, samples), BF16),
        ],
        in_specs=[in_vmem] * 4,
        out_specs=[in_vmem] * 3,
        compiler_params=pltpu.CompilerParams(vmem_limit_bytes=24 * 2**20),
        cost_estimate=pl.CostEstimate(
            flops=4 * 10**9, bytes_accessed=9 * 2**20, transcendentals=0
        ),
        name="prep",
    )(cur, chirp, bins, tables[1])
    factor = 1.0 / float(samples * devices // BINS)
    return pl.pallas_call(
        functools.partial(work_kernel, channels, devices, factor),
        out_shape=jax.ShapeDtypeStruct((channels, 4, BINS // devices), F32),
        in_specs=[in_vmem] * 13,
        out_specs=in_vmem,
        scratch_shapes=[
            pltpu.VMEM((HALF * rows, RADIX), F32),
            pltpu.VMEM((8 * rows, samples), BF16),
            pltpu.VMEM((devices, 8, RADIX), F32),
            pltpu.VMEM((devices, 8, RADIX), F32),
            pltpu.SemaphoreType.DMA((devices,)),
            pltpu.SemaphoreType.DMA((devices,)),
        ],
        compiler_params=pltpu.CompilerParams(
            collective_id=0, has_side_effects=True, vmem_limit_bytes=32 * 2**20
        ),
        name="work",
    )(prev, gain, part, onehot, bins, tables[0], *tables[2:], twist)


def solution(mesh):
    placed = (P("freq", None, "tm"), P("freq", None), P("tm"))
    return jax.shard_map(
        shards, mesh=mesh, in_specs=placed, out_specs=P("freq", None, "tm"), check_vma=False
    )
```

```python
import functools

import jax
import jax.numpy as jnp
import numpy as np
from jax import lax
from jax.experimental import pallas as pl
from jax.experimental.pallas import tpu as pltpu
from jax.sharding import PartitionSpec as P

BINS = 1024
RADIX = 128
HALF = 64
LOW_BINS = 256
F32 = jnp.float32
BF16 = jnp.bfloat16


def split_table(table):
    high = table.astype(jnp.bfloat16)
    low = (table - high.astype(np.float64)).astype(jnp.bfloat16)
    return high, low


def dft_tables():
    index = np.arange(RADIX)
    angle = 2.0 * np.pi * (index[:, None] * index[None, :] % RADIX) / RADIX
    four_real, four_imag = np.cos(angle), -np.sin(angle)
    turn = 2.0 * np.pi * (index[:, None] * index[None, :]) / (RADIX * RADIX)
    twist = np.concatenate([np.cos(turn), -np.sin(turn)], axis=1).astype(np.float32)
    left = np.block([[four_real, -four_imag], [four_imag, four_real]])
    right = np.block([[four_real, four_imag], [-four_imag, four_real]])
    back_right = np.block([[four_real, -four_imag], [four_imag, four_real]]) / RADIX
    kept_real, kept_imag = four_real[HALF:], four_imag[HALF:]
    back_left = np.block([[kept_real, kept_imag], [-kept_imag, kept_real]]) / RADIX
    tables = []
    for part in range(2):
        columns = np.arange(4 * HALF).reshape(4, HALF)[part::2].reshape(-1)
        tables.append(np.concatenate(split_table(left[:, columns]), axis=1))
    for table in (right, back_right, back_left):
        tables.extend(split_table(table))
    return tables, twist


def halves(value):
    high = value.astype(BF16)
    low = (value - high.astype(F32)).astype(BF16)
    return high, low


def dot(a, b):
    return jnp.dot(a, b, preferred_element_type=F32)


def cos_sin(phase):
    half = phase * 0.5
    square = half * half
    sine = half * (
        1.0 + square * (-1.0 / 6 + square * (1.0 / 120 + square * (-1.0 / 5040 + square * (
            1.0 / 362880 + square * (-1.0 / 39916800 + square * (1.0 / 6227020800))))))
    )
    cosine = 1.0 + square * (-1.0 / 2 + square * (1.0 / 24 + square * (-1.0 / 720 + square * (
        1.0 / 40320 + square * (-1.0 / 3628800 + square * (
            1.0 / 479001600 + square * (-1.0 / 87178291200))))))
    )
    return 1.0 - 2.0 * sine * sine, 2.0 * sine * cosine


def paired(block, base, part):
    return jnp.concatenate([block[base + part], block[base + 2 + part]], axis=1)


def first_stage(table, block, base):
    series = jnp.concatenate([paired(block, base, 0), paired(block, base, 1)], axis=0)
    return dot(table[...], jnp.concatenate([series, series], axis=0))


def prep_kernel(sizes, *refs):
    curs, (chirp, bins, left, gain, part, onehot) = refs[:len(sizes)], refs[len(sizes):]
    lane_bins = lax.broadcasted_iota(jnp.int32, (LOW_BINS, 2 * RADIX), 0)

    for chunk, cur in enumerate(curs):
        start = sum(sizes[:chunk])

        def channel(c, carry):
            cosine, sine = cos_sin(chirp[start + c].T)
            gain[start + c] = jnp.concatenate([cosine, sine], axis=1)
            part[start + c] = first_stage(left, cur, 4 * c)
            return carry

        lax.fori_loop(0, sizes[chunk], channel, 0)

    def mark(m, carry):
        own = bins[pl.ds(m, 1), :]
        columns = pl.ds(pl.multiple_of(m * 2 * RADIX, 2 * RADIX), 2 * RADIX)
        onehot[:, columns] = jnp.where(
            lane_bins == own - own // LOW_BINS * LOW_BINS, 1.0, 0.0
        ).astype(BF16)
        return carry

    lax.fori_loop(0, HALF // 2, mark, 0)


def filter_channels(
    start, size, prev, gain, part, left, right_h, right_l, back_right_h, back_right_l,
    back_left_h, back_left_l, twist, stokes,
):
    rows = 4 * size
    twist_real = twist[:, :RADIX]
    twist_imag = twist[:, RADIX:]
    wide_real = jnp.concatenate([twist_real, twist_real], axis=1)
    wide_imag = jnp.concatenate([twist_imag, twist_imag], axis=1)

    def channel(c):
        base = 4 * c
        section = part[start + c] + first_stage(left, prev, base)
        real, imag = section[:RADIX], section[RADIX:]
        turned_real = real * wide_real - imag * wide_imag
        turned_imag = real * wide_imag + imag * wide_real
        gain_real, gain_imag = gain[start + c, :, :RADIX], gain[start + c, :, RADIX:]
        waves_real, waves_imag = [], []
        for p in range(2):
            lanes = slice(p * RADIX, (p + 1) * RADIX)
            high, low = halves(
                jnp.concatenate([turned_real[:, lanes], turned_imag[:, lanes]], axis=1)
            )
            spec = dot(high, right_h[...]) + dot(low, right_h[...]) + dot(high, right_l[...])
            spec_real, spec_imag = spec[:, :RADIX], spec[:, RADIX:]
            high, low = halves(
                jnp.concatenate(
                    [
                        spec_real * gain_real - spec_imag * gain_imag,
                        spec_real * gain_imag + spec_imag * gain_real,
                    ],
                    axis=1,
                )
            )
            back = (
                dot(high, back_right_h[...])
                + dot(low, back_right_h[...])
                + dot(high, back_right_l[...])
            )
            back_real, back_imag = back[:, :RADIX], back[:, RADIX:]
            waves_real.append(back_real * twist_real + back_imag * twist_imag)
            waves_imag.append(back_imag * twist_real - back_real * twist_imag)
        high, low = halves(
            jnp.concatenate(
                [jnp.concatenate(waves_real, axis=1), jnp.concatenate(waves_imag, axis=1)], axis=0
            )
        )
        wave = (
            dot(back_left_h[...], high) + dot(back_left_h[...], low) + dot(back_left_l[...], high)
        )
        xr, xi = wave[:HALF, :RADIX], wave[HALF:, :RADIX]
        yr, yi = wave[:HALF, RADIX:], wave[HALF:, RADIX:]
        first = xr * xr + xi * xi
        second = yr * yr + yi * yi
        stokes[pl.ds(base, HALF, rows), :] = first + second
        stokes[pl.ds(base + 1, HALF, rows), :] = first - second
        stokes[pl.ds(base + 2, HALF, rows), :] = 2.0 * (xr * yr + xi * yi)
        stokes[pl.ds(base + 3, HALF, rows), :] = 2.0 * (xr * yi - xi * yr)

    def channel_pair(i, carry):
        channel(2 * i)
        channel(2 * i + 1)
        return carry

    lax.fori_loop(0, size // 2, channel_pair, 0)


def work_kernel(sizes, devices, factor, *refs):
    ready, refs = refs[:len(sizes) - 1], refs[len(sizes) - 1:]
    onehot, bins, *operands = refs[:13]
    out, last, picked, tiles, landed, send_sems, recv_sems = refs[13:]
    me = lax.axis_index("tm")
    barrier = pltpu.get_barrier_semaphore()

    def greet(i, carry):
        pl.semaphore_signal(
            barrier, inc=1, device_id={"tm": lax.rem(me + i, devices)},
            device_id_type=pl.DeviceIdType.MESH,
        )
        return carry

    lax.fori_loop(1, devices, greet, 0)

    start = sum(sizes[:-1])
    filter_channels(start, sizes[-1], *operands, last)
    stokes = (*ready, last)
    rows = 4 * sum(sizes)
    groups = BINS // LOW_BINS

    def pick(m, carry):
        pieces = []
        for array, size in zip(stokes, sizes):
            count = 4 * size
            at = pl.multiple_of(m * 2 * count, 2 * count)
            pieces.append(
                jnp.concatenate(
                    [array[pl.ds(at, count), :], array[pl.ds(at + count, count), :]], axis=1
                )
            )
        value = jnp.concatenate(pieces, axis=0)
        high = value.astype(BF16).astype(F32)
        both = jnp.concatenate([high, value - high], axis=0)
        group = bins[pl.ds(m, 1), :] // LOW_BINS
        columns = pl.ds(pl.multiple_of(m * 2 * RADIX, 2 * RADIX), 2 * RADIX)
        for q in range(groups):
            picked[pl.ds(q * 2 * rows, 2 * rows), columns] = jnp.where(
                group == q, both, 0.0
            ).astype(BF16)
        return carry

    lax.fori_loop(0, HALF // 2, pick, 0)

    total = lax.dot_general(
        picked[...], onehot[...], (((1,), (1,)), ((), ())), preferred_element_type=F32
    )
    for q in range(groups):
        at = q * 2 * rows
        folded = total[at:at + rows] + total[at + rows:at + 2 * rows]
        for h in range(2):
            for b in range(4):
                lanes = slice(h * RADIX + 32 * b, h * RADIX + 32 * b + 32)
                tiles[q * 8 + h * 4 + b] = jnp.concatenate(
                    [folded[8 * a:8 * a + 8, lanes] for a in range(4)], axis=1
                )

    pl.semaphore_wait(barrier, devices - 1)

    def copy(i):
        peer = lax.rem(me + i, devices)
        return pltpu.make_async_remote_copy(
            src_ref=tiles.at[peer],
            dst_ref=landed.at[i],
            send_sem=send_sems.at[i],
            recv_sem=recv_sems.at[i],
            device_id={"tm": peer},
            device_id_type=pl.DeviceIdType.MESH,
        )

    def send(i, carry):
        copy(i).start()
        return carry

    lax.fori_loop(1, devices, send, 0)

    def take(i, total):
        copy(i).wait_recv()
        return total + landed[i]

    total = lax.fori_loop(1, devices, take, tiles[me]) * factor
    for a in range(4):
        for k in range(2):
            out[2 * a + k] = total[4 * k:4 * k + 4, 32 * a:32 * a + 32]

    def drain(i, carry):
        copy(i).wait_send()
        return carry

    lax.fori_loop(1, devices, drain, 0)


def shards(baseband, chirp_phase, phase_bins):
    channels, _, samples = baseband.shape
    devices = lax.axis_size("tm")
    rows = 4 * channels
    sizes = (channels // 2, channels // 4, channels // 4)
    route = [(i, i + 1) for i in range(devices - 1)]
    curs, prevs = [], []
    for chunk, size in enumerate(sizes):
        start = sum(sizes[:chunk])
        cur = baseband[start:start + size].reshape(4 * size, HALF, RADIX)
        curs.append(cur)
        prevs.append(lax.ppermute(cur, "tm", route))
    chirp = chirp_phase.reshape(channels, RADIX, RADIX)
    bins = phase_bins.reshape(samples // (2 * RADIX), 2 * RADIX)
    tables, twist = dft_tables()
    in_vmem = pl.BlockSpec(memory_space=pltpu.VMEM)
    gain, part, onehot = pl.pallas_call(
        functools.partial(prep_kernel, sizes),
        out_shape=[
            jax.ShapeDtypeStruct((channels, RADIX, 2 * RADIX), F32),
            jax.ShapeDtypeStruct((channels, 2 * RADIX, 2 * RADIX), F32),
            jax.ShapeDtypeStruct((LOW_BINS, samples), BF16),
        ],
        in_specs=[in_vmem] * (len(sizes) + 3),
        out_specs=[in_vmem] * 3,
        compiler_params=pltpu.CompilerParams(vmem_limit_bytes=24 * 2**20),
        cost_estimate=pl.CostEstimate(
            flops=4 * 10**9, bytes_accessed=9 * 2**20, transcendentals=0
        ),
        name="prep",
    )(*curs, chirp, bins, tables[1])
    constants = (tables[0], *tables[2:], twist)
    ready = []
    for chunk, size in enumerate(sizes[:-1]):
        ready.append(
            pl.pallas_call(
                functools.partial(filter_channels, sum(sizes[:chunk]), size),
                out_shape=jax.ShapeDtypeStruct((HALF * 4 * size, RADIX), F32),
                in_specs=[in_vmem] * 11,
                out_specs=in_vmem,
                compiler_params=pltpu.CompilerParams(vmem_limit_bytes=24 * 2**20),
                cost_estimate=pl.CostEstimate(
                    flops=size * 10**9, bytes_accessed=size * 2**20, transcendentals=0
                ),
                name="filter",
            )(prevs[chunk], gain, part, *constants)
        )
    factor = 1.0 / float(samples * devices // BINS)
    return pl.pallas_call(
        functools.partial(work_kernel, sizes, devices, factor),
        out_shape=jax.ShapeDtypeStruct((channels, 4, BINS // devices), F32),
        in_specs=[in_vmem] * (len(ready) + 13),
        out_specs=in_vmem,
        scratch_shapes=[
            pltpu.VMEM((HALF * 4 * sizes[-1], RADIX), F32),
            pltpu.VMEM((8 * rows, samples), BF16),
            pltpu.VMEM((devices, 8, RADIX), F32),
            pltpu.VMEM((devices, 8, RADIX), F32),
            pltpu.SemaphoreType.DMA((devices,)),
            pltpu.SemaphoreType.DMA((devices,)),
        ],
        compiler_params=pltpu.CompilerParams(
            collective_id=0, has_side_effects=True, vmem_limit_bytes=32 * 2**20
        ),
        name="work",
    )(*ready, onehot, bins, prevs[-1], gain, part, *constants)


def solution(mesh):
    placed = (P("freq", None, "tm"), P("freq", None), P("tm"))
    return jax.shard_map(
        shards, mesh=mesh, in_specs=placed, out_specs=P("freq", None, "tm"), check_vma=False
    )
```

```python
import functools

import jax
import jax.numpy as jnp
import numpy as np
from jax import lax
from jax.experimental import pallas as pl
from jax.experimental.pallas import tpu as pltpu
from jax.sharding import PartitionSpec as P

BINS = 1024
RADIX = 128
HALF = 64
LOW_BINS = 256
F32 = jnp.float32
BF16 = jnp.bfloat16


def split_table(table):
    high = table.astype(jnp.bfloat16)
    low = (table - high.astype(np.float64)).astype(jnp.bfloat16)
    return high, low


def dft_tables():
    index = np.arange(RADIX)
    angle = 2.0 * np.pi * (index[:, None] * index[None, :] % RADIX) / RADIX
    four_real, four_imag = np.cos(angle), -np.sin(angle)
    turn = 2.0 * np.pi * (index[:, None] * index[None, :]) / (RADIX * RADIX)
    twist = np.concatenate([np.cos(turn), -np.sin(turn)], axis=1).astype(np.float32)
    left = np.block([[four_real, -four_imag], [four_imag, four_real]])
    right = np.block([[four_real, four_imag], [-four_imag, four_real]])
    back_right = np.block([[four_real, -four_imag], [four_imag, four_real]]) / RADIX
    kept_real, kept_imag = four_real[HALF:], four_imag[HALF:]
    back_left = np.block([[kept_real, kept_imag], [-kept_imag, kept_real]]) / RADIX
    tables = []
    for part in range(2):
        columns = np.arange(4 * HALF).reshape(4, HALF)[part::2].reshape(-1)
        tables.append(np.concatenate(split_table(left[:, columns]), axis=1))
    for table in (right, back_right, back_left):
        tables.extend(split_table(table))
    return tables, twist


def halves(value):
    high = value.astype(BF16)
    low = (value - high.astype(F32)).astype(BF16)
    return high, low


def dot(a, b):
    return jnp.dot(a, b, preferred_element_type=F32)


def cos_sin(phase):
    half = phase * 0.5
    square = half * half
    sine = half * (
        1.0 + square * (-1.0 / 6 + square * (1.0 / 120 + square * (-1.0 / 5040 + square * (
            1.0 / 362880 + square * (-1.0 / 39916800 + square * (1.0 / 6227020800))))))
    )
    cosine = 1.0 + square * (-1.0 / 2 + square * (1.0 / 24 + square * (-1.0 / 720 + square * (
        1.0 / 40320 + square * (-1.0 / 3628800 + square * (
            1.0 / 479001600 + square * (-1.0 / 87178291200))))))
    )
    return 1.0 - 2.0 * sine * sine, 2.0 * sine * cosine


def paired(block, base, part):
    return jnp.concatenate([block[base + part], block[base + 2 + part]], axis=1)


def first_stage(table, block, base):
    series = jnp.concatenate([paired(block, base, 0), paired(block, base, 1)], axis=0)
    return dot(table[...], jnp.concatenate([series, series], axis=0))


def prep_kernel(sizes, *refs):
    curs, (chirp, bins, left, gain, part, onehot) = refs[:len(sizes)], refs[len(sizes):]
    lane_bins = lax.broadcasted_iota(jnp.int32, (LOW_BINS, 2 * RADIX), 0)

    for chunk, cur in enumerate(curs):
        start = sum(sizes[:chunk])

        def channel(c, carry):
            cosine, sine = cos_sin(chirp[start + c].T)
            gain[start + c] = jnp.concatenate([cosine, sine], axis=1)
            part[start + c] = first_stage(left, cur, 4 * c)
            return carry

        lax.fori_loop(0, sizes[chunk], channel, 0)

    def mark(m, carry):
        own = bins[pl.ds(m, 1), :]
        columns = pl.ds(pl.multiple_of(m * 2 * RADIX, 2 * RADIX), 2 * RADIX)
        onehot[:, columns] = jnp.where(
            lane_bins == own - own // LOW_BINS * LOW_BINS, 1.0, 0.0
        ).astype(BF16)
        return carry

    lax.fori_loop(0, HALF // 2, mark, 0)


def filter_channels(
    start, size, prev, gain, part, left, right_h, right_l, back_right_h, back_right_l,
    back_left_h, back_left_l, twist, stokes,
):
    rows = 4 * size
    twist_real = twist[:, :RADIX]
    twist_imag = twist[:, RADIX:]
    wide_real = jnp.concatenate([twist_real, twist_real], axis=1)
    wide_imag = jnp.concatenate([twist_imag, twist_imag], axis=1)

    def channel(c):
        base = 4 * c
        section = part[start + c] + first_stage(left, prev, base)
        real, imag = section[:RADIX], section[RADIX:]
        turned_real = real * wide_real - imag * wide_imag
        turned_imag = real * wide_imag + imag * wide_real
        gain_real, gain_imag = gain[start + c, :, :RADIX], gain[start + c, :, RADIX:]
        waves_real, waves_imag = [], []
        for p in range(2):
            lanes = slice(p * RADIX, (p + 1) * RADIX)
            high, low = halves(
                jnp.concatenate([turned_real[:, lanes], turned_imag[:, lanes]], axis=1)
            )
            spec = dot(high, right_h[...]) + dot(low, right_h[...]) + dot(high, right_l[...])
            spec_real, spec_imag = spec[:, :RADIX], spec[:, RADIX:]
            high, low = halves(
                jnp.concatenate(
                    [
                        spec_real * gain_real - spec_imag * gain_imag,
                        spec_real * gain_imag + spec_imag * gain_real,
                    ],
                    axis=1,
                )
            )
            back = (
                dot(high, back_right_h[...])
                + dot(low, back_right_h[...])
                + dot(high, back_right_l[...])
            )
            back_real, back_imag = back[:, :RADIX], back[:, RADIX:]
            waves_real.append(back_real * twist_real + back_imag * twist_imag)
            waves_imag.append(back_imag * twist_real - back_real * twist_imag)
        high, low = halves(
            jnp.concatenate(
                [jnp.concatenate(waves_real, axis=1), jnp.concatenate(waves_imag, axis=1)], axis=0
            )
        )
        wave = (
            dot(back_left_h[...], high) + dot(back_left_h[...], low) + dot(back_left_l[...], high)
        )
        xr, xi = wave[:HALF, :RADIX], wave[HALF:, :RADIX]
        yr, yi = wave[:HALF, RADIX:], wave[HALF:, RADIX:]
        first = xr * xr + xi * xi
        second = yr * yr + yi * yi
        stokes[pl.ds(base, HALF, rows), :] = first + second
        stokes[pl.ds(base + 1, HALF, rows), :] = first - second
        stokes[pl.ds(base + 2, HALF, rows), :] = 2.0 * (xr * yr + xi * yi)
        stokes[pl.ds(base + 3, HALF, rows), :] = 2.0 * (xr * yi - xi * yr)

    def channel_pair(i, carry):
        channel(2 * i)
        channel(2 * i + 1)
        return carry

    lax.fori_loop(0, size // 2, channel_pair, 0)


def work_kernel(sizes, devices, factor, *refs):
    ready, refs = refs[:len(sizes) - 1], refs[len(sizes) - 1:]
    onehot, bins, *operands = refs[:13]
    out, last, picked, tiles, swapped, sums, landed, *sems = refs[13:]
    swap_sems, send_sems, recv_sems = sems
    me = lax.axis_index("tm")
    barrier = pltpu.get_barrier_semaphore()

    chips = devices // 2
    half = chips // 2
    core, chip = lax.rem(me, 2), me // 2
    side, place = chip // half, lax.rem(chip, half)
    partner = me + 1 - 2 * core

    def peer_chip(i):
        other = lax.rem(side + 1 - i // half, 2)
        return other * half + lax.rem(place + i, half)

    def greet(device):
        pl.semaphore_signal(
            barrier, inc=1, device_id={"tm": device}, device_id_type=pl.DeviceIdType.MESH
        )

    def greet_chip(i, carry):
        greet(peer_chip(i) * 2 + core)
        return carry

    steps = [(0, half), (half + 1, chips)]
    for low, high in steps:
        lax.fori_loop(low, high, greet_chip, 0)
    greet(partner)

    start = sum(sizes[:-1])
    filter_channels(start, sizes[-1], *operands, last)
    stokes = (*ready, last)
    rows = 4 * sum(sizes)
    groups = BINS // LOW_BINS

    def pick(m, carry):
        pieces = []
        for array, size in zip(stokes, sizes):
            count = 4 * size
            at = pl.multiple_of(m * 2 * count, 2 * count)
            pieces.append(
                jnp.concatenate(
                    [array[pl.ds(at, count), :], array[pl.ds(at + count, count), :]], axis=1
                )
            )
        value = jnp.concatenate(pieces, axis=0)
        high = value.astype(BF16).astype(F32)
        both = jnp.concatenate([high, value - high], axis=0)
        group = bins[pl.ds(m, 1), :] // LOW_BINS
        columns = pl.ds(pl.multiple_of(m * 2 * RADIX, 2 * RADIX), 2 * RADIX)
        for q in range(groups):
            picked[pl.ds(q * 2 * rows, 2 * rows), columns] = jnp.where(
                group == q, both, 0.0
            ).astype(BF16)
        return carry

    lax.fori_loop(0, HALF // 2, pick, 0, unroll=4)

    total = lax.dot_general(
        picked[...], onehot[...], (((1,), (1,)), ((), ())), preferred_element_type=F32
    )
    for q in range(groups):
        at = q * 2 * rows
        folded = total[at:at + rows] + total[at + rows:at + 2 * rows]
        for h in range(2):
            for b in range(4):
                lanes = slice(h * RADIX + 32 * b, h * RADIX + 32 * b + 32)
                tiles[b % 2, q * 4 + h * 2 + b // 2] = jnp.concatenate(
                    [folded[8 * a:8 * a + 8, lanes] for a in range(4)], axis=1
                )

    pl.semaphore_wait(barrier, chips)

    swap = pltpu.make_async_remote_copy(
        src_ref=tiles.at[1 - core],
        dst_ref=swapped,
        send_sem=swap_sems.at[0],
        recv_sem=swap_sems.at[1],
        device_id={"tm": partner},
        device_id_type=pl.DeviceIdType.MESH,
    )
    swap.start()
    swap.wait_recv()
    sums[...] = tiles[core] + swapped[...]

    def copy(i):
        peer = peer_chip(i)
        return pltpu.make_async_remote_copy(
            src_ref=sums.at[peer],
            dst_ref=landed.at[i],
            send_sem=send_sems.at[i],
            recv_sem=recv_sems.at[i],
            device_id={"tm": peer * 2 + core},
            device_id_type=pl.DeviceIdType.MESH,
        )

    def send(i, carry):
        copy(i).start()
        return carry

    def take(i, total):
        copy(i).wait_recv()
        return total + landed[i]

    for low, high in steps:
        lax.fori_loop(low, high, send, 0)
    total = sums[chip]
    for low, high in reversed(steps):
        total = lax.fori_loop(low, high, take, total)
    total = total * factor
    for a in range(4):
        for k in range(2):
            out[2 * a + k] = total[4 * k:4 * k + 4, 32 * a:32 * a + 32]

    swap.wait_send()

    def drain(i, carry):
        copy(i).wait_send()
        return carry

    for low, high in steps:
        lax.fori_loop(low, high, drain, 0)


def shards(baseband, chirp_phase, phase_bins):
    channels, _, samples = baseband.shape
    devices = lax.axis_size("tm")
    rows = 4 * channels
    sizes = (channels // 2, channels // 2)
    route = [(i, i + 1) for i in range(devices - 1)]
    curs, prevs = [], []
    for chunk, size in enumerate(sizes):
        start = sum(sizes[:chunk])
        cur = baseband[start:start + size].reshape(4 * size, HALF, RADIX)
        curs.append(cur)
        prevs.append(lax.ppermute(cur, "tm", route))
    chirp = chirp_phase.reshape(channels, RADIX, RADIX)
    bins = phase_bins.reshape(samples // (2 * RADIX), 2 * RADIX)
    tables, twist = dft_tables()
    in_vmem = pl.BlockSpec(memory_space=pltpu.VMEM)
    gain, part, onehot = pl.pallas_call(
        functools.partial(prep_kernel, sizes),
        out_shape=[
            jax.ShapeDtypeStruct((channels, RADIX, 2 * RADIX), F32),
            jax.ShapeDtypeStruct((channels, 2 * RADIX, 2 * RADIX), F32),
            jax.ShapeDtypeStruct((LOW_BINS, samples), BF16),
        ],
        in_specs=[in_vmem] * (len(sizes) + 3),
        out_specs=[in_vmem] * 3,
        compiler_params=pltpu.CompilerParams(vmem_limit_bytes=24 * 2**20),
        cost_estimate=pl.CostEstimate(
            flops=4 * 10**9, bytes_accessed=9 * 2**20, transcendentals=0
        ),
        name="prep",
    )(*curs, chirp, bins, tables[1])
    constants = (tables[0], *tables[2:], twist)
    ready = []
    for chunk, size in enumerate(sizes[:-1]):
        ready.append(
            pl.pallas_call(
                functools.partial(filter_channels, sum(sizes[:chunk]), size),
                out_shape=jax.ShapeDtypeStruct((HALF * 4 * size, RADIX), F32),
                in_specs=[in_vmem] * 11,
                out_specs=in_vmem,
                compiler_params=pltpu.CompilerParams(vmem_limit_bytes=24 * 2**20),
                cost_estimate=pl.CostEstimate(
                    flops=size * 10**9, bytes_accessed=size * 2**20, transcendentals=0
                ),
                name="filter",
            )(prevs[chunk], gain, part, *constants)
        )
    factor = 1.0 / float(samples * devices // BINS)
    return pl.pallas_call(
        functools.partial(work_kernel, sizes, devices, factor),
        out_shape=jax.ShapeDtypeStruct((channels, 4, BINS // devices), F32),
        in_specs=[in_vmem] * (len(ready) + 13),
        out_specs=in_vmem,
        scratch_shapes=[
            pltpu.VMEM((HALF * 4 * sizes[-1], RADIX), F32),
            pltpu.VMEM((8 * rows, samples), BF16),
            pltpu.VMEM((2, devices // 2, 8, RADIX), F32),
            pltpu.VMEM((devices // 2, 8, RADIX), F32),
            pltpu.VMEM((devices // 2, 8, RADIX), F32),
            pltpu.VMEM((devices // 2, 8, RADIX), F32),
            pltpu.SemaphoreType.DMA((2,)),
            pltpu.SemaphoreType.DMA((devices // 2,)),
            pltpu.SemaphoreType.DMA((devices // 2,)),
        ],
        compiler_params=pltpu.CompilerParams(
            collective_id=0, has_side_effects=True, vmem_limit_bytes=32 * 2**20
        ),
        name="work",
    )(*ready, onehot, bins, prevs[-1], gain, part, *constants)


def solution(mesh):
    placed = (P("freq", None, "tm"), P("freq", None), P("tm"))
    return jax.shard_map(
        shards, mesh=mesh, in_specs=placed, out_specs=P("freq", None, "tm"), check_vma=False
    )
```

```python
import functools

import jax
import jax.numpy as jnp
import numpy as np
from jax import lax
from jax.experimental import pallas as pl
from jax.experimental.pallas import tpu as pltpu
from jax.sharding import PartitionSpec as P

BINS = 1024
RADIX = 128
HALF = 64
LOW_BINS = 256
F32 = jnp.float32
BF16 = jnp.bfloat16


def split_table(table):
    high = table.astype(jnp.bfloat16)
    low = (table - high.astype(np.float64)).astype(jnp.bfloat16)
    return high, low


def dft_tables():
    index = np.arange(RADIX)
    angle = 2.0 * np.pi * (index[:, None] * index[None, :] % RADIX) / RADIX
    four_real, four_imag = np.cos(angle), -np.sin(angle)
    turn = 2.0 * np.pi * (index[:, None] * index[None, :]) / (RADIX * RADIX)
    twist = np.concatenate([np.cos(turn), -np.sin(turn)], axis=1).astype(np.float32)
    left = np.block([[four_real, -four_imag], [four_imag, four_real]])
    right = np.block([[four_real, four_imag], [-four_imag, four_real]])
    back_right = np.block([[four_real, -four_imag], [four_imag, four_real]]) / RADIX
    kept_real, kept_imag = four_real[HALF:], four_imag[HALF:]
    back_left = np.block([[kept_real, kept_imag], [-kept_imag, kept_real]]) / RADIX
    tables = []
    for part in range(2):
        columns = np.arange(4 * HALF).reshape(4, HALF)[part::2].reshape(-1)
        tables.append(np.concatenate(split_table(left[:, columns]), axis=1))
    for table in (right, back_right):
        tables.extend(split_table(table))
    tables.append(np.concatenate(split_table(back_left), axis=0))
    return tables, twist


def halves(value):
    high = value.astype(BF16)
    low = (value - high.astype(F32)).astype(BF16)
    return high, low


def dot(a, b):
    return jnp.dot(a, b, preferred_element_type=F32)


def cos_sin(phase):
    half = phase * 0.5
    square = half * half
    sine = half * (
        1.0 + square * (-1.0 / 6 + square * (1.0 / 120 + square * (-1.0 / 5040 + square * (
            1.0 / 362880 + square * (-1.0 / 39916800 + square * (1.0 / 6227020800))))))
    )
    cosine = 1.0 + square * (-1.0 / 2 + square * (1.0 / 24 + square * (-1.0 / 720 + square * (
        1.0 / 40320 + square * (-1.0 / 3628800 + square * (
            1.0 / 479001600 + square * (-1.0 / 87178291200))))))
    )
    return 1.0 - 2.0 * sine * sine, 2.0 * sine * cosine


def paired(block, base, part):
    return jnp.concatenate([block[base + part], block[base + 2 + part]], axis=1)


def first_stage(table, block, base):
    series = jnp.concatenate([paired(block, base, 0), paired(block, base, 1)], axis=0)
    return dot(table[...], jnp.concatenate([series, series], axis=0))


def prep_kernel(sizes, *refs):
    curs, (chirp, bins, left, gain, part, onehot) = refs[:len(sizes)], refs[len(sizes):]
    lane_bins = lax.broadcasted_iota(jnp.int32, (LOW_BINS, 2 * RADIX), 0)

    for chunk, cur in enumerate(curs):
        start = sum(sizes[:chunk])

        def channel(c, carry):
            cosine, sine = cos_sin(chirp[start + c].T)
            gain[start + c] = jnp.concatenate([cosine, sine], axis=1)
            part[start + c] = first_stage(left, cur, 4 * c)
            return carry

        lax.fori_loop(0, sizes[chunk], channel, 0)

    def mark(m, carry):
        own = bins[pl.ds(m, 1), :]
        columns = pl.ds(pl.multiple_of(m * 2 * RADIX, 2 * RADIX), 2 * RADIX)
        onehot[:, columns] = jnp.where(
            lane_bins == own - own // LOW_BINS * LOW_BINS, 1.0, 0.0
        ).astype(BF16)
        return carry

    lax.fori_loop(0, HALF // 2, mark, 0)


def filter_channels(
    start, size, prev, gain, part, left, right_h, right_l, back_right_h, back_right_l,
    back_left, twist, stokes,
):
    rows = 4 * size
    twist_real = twist[:, :RADIX]
    twist_imag = twist[:, RADIX:]
    wide_real = jnp.concatenate([twist_real, twist_real], axis=1)
    wide_imag = jnp.concatenate([twist_imag, twist_imag], axis=1)

    def twice(value):
        return jnp.concatenate([value, value], axis=0)

    tall_real, tall_imag = twice(twist_real), twice(twist_imag)

    def channel(c):
        base = 4 * c
        section = part[start + c] + first_stage(left, prev, base)
        real, imag = section[:RADIX], section[RADIX:]
        turned_real = real * wide_real - imag * wide_imag
        turned_imag = real * wide_imag + imag * wide_real
        gain_real, gain_imag = twice(gain[start + c, :, :RADIX]), twice(gain[start + c, :, RADIX:])
        high, low = halves(
            jnp.concatenate(
                [
                    jnp.concatenate([turned_real[:, :RADIX], turned_imag[:, :RADIX]], axis=1),
                    jnp.concatenate([turned_real[:, RADIX:], turned_imag[:, RADIX:]], axis=1),
                ],
                axis=0,
            )
        )
        spec = dot(high, right_h[...]) + dot(low, right_h[...]) + dot(high, right_l[...])
        spec_real, spec_imag = spec[:, :RADIX], spec[:, RADIX:]
        high, low = halves(
            jnp.concatenate(
                [
                    spec_real * gain_real - spec_imag * gain_imag,
                    spec_real * gain_imag + spec_imag * gain_real,
                ],
                axis=1,
            )
        )
        back = (
            dot(high, back_right_h[...])
            + dot(low, back_right_h[...])
            + dot(high, back_right_l[...])
        )
        back_real, back_imag = back[:, :RADIX], back[:, RADIX:]
        wave_real = back_real * tall_real + back_imag * tall_imag
        wave_imag = back_imag * tall_real - back_real * tall_imag
        high, low = halves(
            jnp.concatenate(
                [
                    jnp.concatenate([wave_real[:RADIX], wave_imag[:RADIX]], axis=0),
                    jnp.concatenate([wave_real[RADIX:], wave_imag[RADIX:]], axis=0),
                ],
                axis=1,
            )
        )
        both = dot(back_left[...], high)
        wave = both[:RADIX] + both[RADIX:] + dot(back_left[:RADIX, :], low)
        xr, xi = wave[:HALF, :RADIX], wave[HALF:, :RADIX]
        yr, yi = wave[:HALF, RADIX:], wave[HALF:, RADIX:]
        first = xr * xr + xi * xi
        second = yr * yr + yi * yi
        stokes[pl.ds(base, HALF, rows), :] = first + second
        stokes[pl.ds(base + 1, HALF, rows), :] = first - second
        stokes[pl.ds(base + 2, HALF, rows), :] = 2.0 * (xr * yr + xi * yi)
        stokes[pl.ds(base + 3, HALF, rows), :] = 2.0 * (xr * yi - xi * yr)

    def channel_pair(i, carry):
        channel(2 * i)
        channel(2 * i + 1)
        return carry

    lax.fori_loop(0, size // 2, channel_pair, 0)


def work_kernel(sizes, devices, factor, *refs):
    ready, refs = refs[:len(sizes) - 1], refs[len(sizes) - 1:]
    onehot, bins, *operands = refs[:12]
    out, last, picked, tiles, swapped, sums, landed, *sems = refs[12:]
    swap_sems, send_sems, recv_sems = sems
    me = lax.axis_index("tm")
    barrier = pltpu.get_barrier_semaphore()

    chips = devices // 2
    half = chips // 2
    core, chip = lax.rem(me, 2), me // 2
    side, place = chip // half, lax.rem(chip, half)
    partner = me + 1 - 2 * core

    def peer_chip(i):
        other = lax.rem(side + 1 - i // half, 2)
        return other * half + lax.rem(place + i, half)

    def greet(device):
        pl.semaphore_signal(
            barrier, inc=1, device_id={"tm": device}, device_id_type=pl.DeviceIdType.MESH
        )

    def greet_chip(i, carry):
        greet(peer_chip(i) * 2 + core)
        return carry

    steps = [(0, half), (half + 1, chips)]
    for low, high in steps:
        lax.fori_loop(low, high, greet_chip, 0)
    greet(partner)

    start = sum(sizes[:-1])
    filter_channels(start, sizes[-1], *operands, last)
    stokes = (*ready, last)
    rows = 4 * sum(sizes)
    groups = BINS // LOW_BINS

    def pick(m, carry):
        pieces = []
        for array, size in zip(stokes, sizes):
            count = 4 * size
            at = pl.multiple_of(m * 2 * count, 2 * count)
            pieces.append(
                jnp.concatenate(
                    [array[pl.ds(at, count), :], array[pl.ds(at + count, count), :]], axis=1
                )
            )
        value = jnp.concatenate(pieces, axis=0)
        high = value.astype(BF16).astype(F32)
        both = jnp.concatenate([high, value - high], axis=0)
        group = bins[pl.ds(m, 1), :] // LOW_BINS
        columns = pl.ds(pl.multiple_of(m * 2 * RADIX, 2 * RADIX), 2 * RADIX)
        for q in range(groups):
            picked[pl.ds(q * 2 * rows, 2 * rows), columns] = jnp.where(
                group == q, both, 0.0
            ).astype(BF16)
        return carry

    lax.fori_loop(0, HALF // 2, pick, 0, unroll=4)

    total = lax.dot_general(
        picked[...], onehot[...], (((1,), (1,)), ((), ())), preferred_element_type=F32
    )
    for q in range(groups):
        at = q * 2 * rows
        folded = total[at:at + rows] + total[at + rows:at + 2 * rows]
        for h in range(2):
            for b in range(4):
                lanes = slice(h * RADIX + 32 * b, h * RADIX + 32 * b + 32)
                tiles[b % 2, q * 4 + h * 2 + b // 2] = jnp.concatenate(
                    [folded[8 * a:8 * a + 8, lanes] for a in range(4)], axis=1
                )

    pl.semaphore_wait(barrier, chips)

    swap = pltpu.make_async_remote_copy(
        src_ref=tiles.at[1 - core],
        dst_ref=swapped,
        send_sem=swap_sems.at[0],
        recv_sem=swap_sems.at[1],
        device_id={"tm": partner},
        device_id_type=pl.DeviceIdType.MESH,
    )
    swap.start()
    swap.wait_recv()
    sums[...] = tiles[core] + swapped[...]

    def copy(i):
        peer = peer_chip(i)
        return pltpu.make_async_remote_copy(
            src_ref=sums.at[peer],
            dst_ref=landed.at[i],
            send_sem=send_sems.at[i],
            recv_sem=recv_sems.at[i],
            device_id={"tm": peer * 2 + core},
            device_id_type=pl.DeviceIdType.MESH,
        )

    def send(i, carry):
        copy(i).start()
        return carry

    def take(i, total):
        copy(i).wait_recv()
        return total + landed[i]

    for low, high in steps:
        lax.fori_loop(low, high, send, 0)
    total = sums[chip]
    for low, high in reversed(steps):
        total = lax.fori_loop(low, high, take, total)
    total = total * factor
    for a in range(4):
        for k in range(2):
            out[2 * a + k] = total[4 * k:4 * k + 4, 32 * a:32 * a + 32]

    swap.wait_send()

    def drain(i, carry):
        copy(i).wait_send()
        return carry

    for low, high in steps:
        lax.fori_loop(low, high, drain, 0)


def shards(baseband, chirp_phase, phase_bins):
    channels, _, samples = baseband.shape
    devices = lax.axis_size("tm")
    rows = 4 * channels
    sizes = (channels // 2, channels // 2)
    route = [(i, i + 1) for i in range(devices - 1)]
    curs, prevs = [], []
    for chunk, size in enumerate(sizes):
        start = sum(sizes[:chunk])
        cur = baseband[start:start + size].reshape(4 * size, HALF, RADIX)
        curs.append(cur)
        prevs.append(lax.ppermute(cur, "tm", route))
    chirp = chirp_phase.reshape(channels, RADIX, RADIX)
    bins = phase_bins.reshape(samples // (2 * RADIX), 2 * RADIX)
    tables, twist = dft_tables()
    in_vmem = pl.BlockSpec(memory_space=pltpu.VMEM)
    gain, part, onehot = pl.pallas_call(
        functools.partial(prep_kernel, sizes),
        out_shape=[
            jax.ShapeDtypeStruct((channels, RADIX, 2 * RADIX), F32),
            jax.ShapeDtypeStruct((channels, 2 * RADIX, 2 * RADIX), F32),
            jax.ShapeDtypeStruct((LOW_BINS, samples), BF16),
        ],
        in_specs=[in_vmem] * (len(sizes) + 3),
        out_specs=[in_vmem] * 3,
        compiler_params=pltpu.CompilerParams(vmem_limit_bytes=24 * 2**20),
        cost_estimate=pl.CostEstimate(
            flops=4 * 10**9, bytes_accessed=9 * 2**20, transcendentals=0
        ),
        name="prep",
    )(*curs, chirp, bins, tables[1])
    constants = (tables[0], *tables[2:], twist)
    ready = []
    for chunk, size in enumerate(sizes[:-1]):
        ready.append(
            pl.pallas_call(
                functools.partial(filter_channels, sum(sizes[:chunk]), size),
                out_shape=jax.ShapeDtypeStruct((HALF * 4 * size, RADIX), F32),
                in_specs=[in_vmem] * 10,
                out_specs=in_vmem,
                compiler_params=pltpu.CompilerParams(vmem_limit_bytes=24 * 2**20),
                cost_estimate=pl.CostEstimate(
                    flops=size * 10**9, bytes_accessed=size * 2**20, transcendentals=0
                ),
                name="filter",
            )(prevs[chunk], gain, part, *constants)
        )
    factor = 1.0 / float(samples * devices // BINS)
    return pl.pallas_call(
        functools.partial(work_kernel, sizes, devices, factor),
        out_shape=jax.ShapeDtypeStruct((channels, 4, BINS // devices), F32),
        in_specs=[in_vmem] * (len(ready) + 12),
        out_specs=in_vmem,
        scratch_shapes=[
            pltpu.VMEM((HALF * 4 * sizes[-1], RADIX), F32),
            pltpu.VMEM((8 * rows, samples), BF16),
            pltpu.VMEM((2, devices // 2, 8, RADIX), F32),
            pltpu.VMEM((devices // 2, 8, RADIX), F32),
            pltpu.VMEM((devices // 2, 8, RADIX), F32),
            pltpu.VMEM((devices // 2, 8, RADIX), F32),
            pltpu.SemaphoreType.DMA((2,)),
            pltpu.SemaphoreType.DMA((devices // 2,)),
            pltpu.SemaphoreType.DMA((devices // 2,)),
        ],
        compiler_params=pltpu.CompilerParams(
            collective_id=0, has_side_effects=True, vmem_limit_bytes=32 * 2**20
        ),
        name="work",
    )(*ready, onehot, bins, prevs[-1], gain, part, *constants)


def solution(mesh):
    placed = (P("freq", None, "tm"), P("freq", None), P("tm"))
    return jax.shard_map(
        shards, mesh=mesh, in_specs=placed, out_specs=P("freq", None, "tm"), check_vma=False
    )
```

```python
import functools

import jax
import jax.numpy as jnp
import numpy as np
from jax import lax
from jax.experimental import pallas as pl
from jax.experimental.pallas import tpu as pltpu
from jax.sharding import PartitionSpec as P

BINS = 1024
RADIX = 128
HALF = 64
LOW_BINS = 256
F32 = jnp.float32
BF16 = jnp.bfloat16


def split_table(table):
    high = table.astype(jnp.bfloat16)
    low = (table - high.astype(np.float64)).astype(jnp.bfloat16)
    return high, low


def dft_tables():
    index = np.arange(RADIX)
    angle = 2.0 * np.pi * (index[:, None] * index[None, :] % RADIX) / RADIX
    four_real, four_imag = np.cos(angle), -np.sin(angle)
    turn = 2.0 * np.pi * (index[:, None] * index[None, :]) / (RADIX * RADIX)
    twist = np.concatenate([np.cos(turn), -np.sin(turn)], axis=1).astype(np.float32)
    left = np.block([[four_real, -four_imag], [four_imag, four_real]])
    right = np.block([[four_real, four_imag], [-four_imag, four_real]])
    back_right = np.block([[four_real, -four_imag], [four_imag, four_real]]) / RADIX
    kept_real, kept_imag = four_real[HALF:], four_imag[HALF:]
    back_left = np.block([[kept_real, kept_imag], [-kept_imag, kept_real]]) / RADIX
    tables = []
    for part in range(2):
        columns = np.arange(4 * HALF).reshape(4, HALF)[part::2].reshape(-1)
        tables.append(np.concatenate(split_table(left[:, columns]), axis=1))
    for table in (right, back_right, back_left):
        tables.extend(split_table(table))
    return tables, twist


def halves(value):
    high = value.astype(BF16)
    low = (value - high.astype(F32)).astype(BF16)
    return high, low


def dot(a, b):
    return jnp.dot(a, b, preferred_element_type=F32)


def cos_sin(phase):
    half = phase * 0.5
    square = half * half
    sine = half * (
        1.0 + square * (-1.0 / 6 + square * (1.0 / 120 + square * (-1.0 / 5040 + square * (
            1.0 / 362880 + square * (-1.0 / 39916800 + square * (1.0 / 6227020800))))))
    )
    cosine = 1.0 + square * (-1.0 / 2 + square * (1.0 / 24 + square * (-1.0 / 720 + square * (
        1.0 / 40320 + square * (-1.0 / 3628800 + square * (
            1.0 / 479001600 + square * (-1.0 / 87178291200))))))
    )
    return 1.0 - 2.0 * sine * sine, 2.0 * sine * cosine


def paired(block, base, part):
    return jnp.concatenate([block[base + part], block[base + 2 + part]], axis=1)


def first_stage(table, block, base):
    series = jnp.concatenate([paired(block, base, 0), paired(block, base, 1)], axis=0)
    return dot(table[...], jnp.concatenate([series, series], axis=0))


def prep_kernel(sizes, *refs):
    curs, (chirp, bins, left, gain, part, onehot) = refs[:len(sizes)], refs[len(sizes):]
    lane_bins = lax.broadcasted_iota(jnp.int32, (LOW_BINS, 2 * RADIX), 0)

    for chunk, cur in enumerate(curs):
        start = sum(sizes[:chunk])

        def channel(c, carry):
            cosine, sine = cos_sin(chirp[start + c].T)
            gain[start + c] = jnp.concatenate([cosine, sine], axis=1)
            part[start + c] = first_stage(left, cur, 4 * c)
            return carry

        lax.fori_loop(0, sizes[chunk], channel, 0)

    def mark(m, carry):
        own = bins[pl.ds(m, 1), :]
        columns = pl.ds(pl.multiple_of(m * 2 * RADIX, 2 * RADIX), 2 * RADIX)
        onehot[:, columns] = jnp.where(
            lane_bins == own - own // LOW_BINS * LOW_BINS, 1.0, 0.0
        ).astype(BF16)
        return carry

    lax.fori_loop(0, HALF // 2, mark, 0)


def filter_channels(
    start, size, prev, gain, part, left, right_h, right_l, back_right_h, back_right_l,
    back_left_h, back_left_l, twist, stokes,
):
    rows = 4 * size
    twist_real = twist[:, :RADIX]
    twist_imag = twist[:, RADIX:]
    wide_real = jnp.concatenate([twist_real, twist_real], axis=1)
    wide_imag = jnp.concatenate([twist_imag, twist_imag], axis=1)

    def channel(c):
        base = 4 * c
        section = part[start + c] + first_stage(left, prev, base)
        real, imag = section[:RADIX], section[RADIX:]
        turned_real = real * wide_real - imag * wide_imag
        turned_imag = real * wide_imag + imag * wide_real
        gain_real, gain_imag = gain[start + c, :, :RADIX], gain[start + c, :, RADIX:]
        waves_real, waves_imag = [], []
        for p in range(2):
            lanes = slice(p * RADIX, (p + 1) * RADIX)
            high, low = halves(
                jnp.concatenate([turned_real[:, lanes], turned_imag[:, lanes]], axis=1)
            )
            spec = dot(high, right_h[...]) + dot(low, right_h[...]) + dot(high, right_l[...])
            spec_real, spec_imag = spec[:, :RADIX], spec[:, RADIX:]
            high, low = halves(
                jnp.concatenate(
                    [
                        spec_real * gain_real - spec_imag * gain_imag,
                        spec_real * gain_imag + spec_imag * gain_real,
                    ],
                    axis=1,
                )
            )
            back = (
                dot(high, back_right_h[...])
                + dot(low, back_right_h[...])
                + dot(high, back_right_l[...])
            )
            back_real, back_imag = back[:, :RADIX], back[:, RADIX:]
            waves_real.append(back_real * twist_real + back_imag * twist_imag)
            waves_imag.append(back_imag * twist_real - back_real * twist_imag)
        high, low = halves(
            jnp.concatenate(
                [jnp.concatenate(waves_real, axis=1), jnp.concatenate(waves_imag, axis=1)], axis=0
            )
        )
        wave = (
            dot(back_left_h[...], high) + dot(back_left_h[...], low) + dot(back_left_l[...], high)
        )
        xr, xi = wave[:HALF, :RADIX], wave[HALF:, :RADIX]
        yr, yi = wave[:HALF, RADIX:], wave[HALF:, RADIX:]
        first = xr * xr + xi * xi
        second = yr * yr + yi * yi
        stokes[pl.ds(base, HALF, rows), :] = first + second
        stokes[pl.ds(base + 1, HALF, rows), :] = first - second
        stokes[pl.ds(base + 2, HALF, rows), :] = 2.0 * (xr * yr + xi * yi)
        stokes[pl.ds(base + 3, HALF, rows), :] = 2.0 * (xr * yi - xi * yr)

    def channel_group(i, carry):
        for step in range(4):
            channel(4 * i + step)
        return carry

    lax.fori_loop(0, size // 4, channel_group, 0)


def work_kernel(sizes, devices, factor, *refs):
    ready, refs = refs[:len(sizes) - 1], refs[len(sizes) - 1:]
    onehot, bins, *operands = refs[:13]
    out, last, picked, tiles, swapped, sums, landed, *sems = refs[13:]
    swap_sems, send_sems, recv_sems = sems
    me = lax.axis_index("tm")
    barrier = pltpu.get_barrier_semaphore()

    chips = devices // 2
    half = chips // 2
    core, chip = lax.rem(me, 2), me // 2
    side, place = chip // half, lax.rem(chip, half)
    partner = me + 1 - 2 * core

    def peer_chip(i):
        other = lax.rem(side + 1 - i // half, 2)
        return other * half + lax.rem(place + i, half)

    def greet(device):
        pl.semaphore_signal(
            barrier, inc=1, device_id={"tm": device}, device_id_type=pl.DeviceIdType.MESH
        )

    def greet_chip(i, carry):
        greet(peer_chip(i) * 2 + core)
        return carry

    steps = [(0, half), (half + 1, chips)]
    for low, high in steps:
        lax.fori_loop(low, high, greet_chip, 0)
    greet(partner)

    start = sum(sizes[:-1])
    filter_channels(start, sizes[-1], *operands, last)
    stokes = (*ready, last)
    rows = 4 * sum(sizes)
    groups = BINS // LOW_BINS

    def pick(m, carry):
        pieces = []
        for array, size in zip(stokes, sizes):
            count = 4 * size
            at = pl.multiple_of(m * 2 * count, 2 * count)
            pieces.append(
                jnp.concatenate(
                    [array[pl.ds(at, count), :], array[pl.ds(at + count, count), :]], axis=1
                )
            )
        value = jnp.concatenate(pieces, axis=0)
        high = value.astype(BF16).astype(F32)
        both = jnp.concatenate([high, value - high], axis=0)
        group = bins[pl.ds(m, 1), :] // LOW_BINS
        columns = pl.ds(pl.multiple_of(m * 2 * RADIX, 2 * RADIX), 2 * RADIX)
        for q in range(groups):
            picked[pl.ds(q * 2 * rows, 2 * rows), columns] = jnp.where(
                group == q, both, 0.0
            ).astype(BF16)
        return carry

    lax.fori_loop(0, HALF // 2, pick, 0, unroll=8)

    total = lax.dot_general(
        picked[...], onehot[...], (((1,), (1,)), ((), ())), preferred_element_type=F32
    )
    for q in range(groups):
        at = q * 2 * rows
        folded = total[at:at + rows] + total[at + rows:at + 2 * rows]
        for h in range(2):
            for b in range(4):
                lanes = slice(h * RADIX + 32 * b, h * RADIX + 32 * b + 32)
                tiles[b % 2, q * 4 + h * 2 + b // 2] = jnp.concatenate(
                    [folded[8 * a:8 * a + 8, lanes] for a in range(4)], axis=1
                )

    pl.semaphore_wait(barrier, chips)

    swap = pltpu.make_async_remote_copy(
        src_ref=tiles.at[1 - core],
        dst_ref=swapped,
        send_sem=swap_sems.at[0],
        recv_sem=swap_sems.at[1],
        device_id={"tm": partner},
        device_id_type=pl.DeviceIdType.MESH,
    )
    swap.start()
    swap.wait_recv()
    sums[...] = tiles[core] + swapped[...]

    def copy(i):
        peer = peer_chip(i)
        return pltpu.make_async_remote_copy(
            src_ref=sums.at[peer],
            dst_ref=landed.at[i],
            send_sem=send_sems.at[i],
            recv_sem=recv_sems.at[i],
            device_id={"tm": peer * 2 + core},
            device_id_type=pl.DeviceIdType.MESH,
        )

    def send(i, carry):
        copy(i).start()
        return carry

    def take(i, total):
        copy(i).wait_recv()
        return total + landed[i]

    for low, high in steps:
        lax.fori_loop(low, high, send, 0)
    total = sums[chip]
    for low, high in reversed(steps):
        total = lax.fori_loop(low, high, take, total)
    total = total * factor
    for a in range(4):
        for k in range(2):
            out[2 * a + k] = total[4 * k:4 * k + 4, 32 * a:32 * a + 32]

    swap.wait_send()

    def drain(i, carry):
        copy(i).wait_send()
        return carry

    for low, high in steps:
        lax.fori_loop(low, high, drain, 0)


def shards(baseband, chirp_phase, phase_bins):
    channels, _, samples = baseband.shape
    devices = lax.axis_size("tm")
    rows = 4 * channels
    sizes = (channels // 2, channels // 2)
    route = [(i, i + 1) for i in range(devices - 1)]
    curs, prevs = [], []
    for chunk, size in enumerate(sizes):
        start = sum(sizes[:chunk])
        cur = baseband[start:start + size].reshape(4 * size, HALF, RADIX)
        curs.append(cur)
        prevs.append(lax.ppermute(cur, "tm", route))
    chirp = chirp_phase.reshape(channels, RADIX, RADIX)
    bins = phase_bins.reshape(samples // (2 * RADIX), 2 * RADIX)
    tables, twist = dft_tables()
    in_vmem = pl.BlockSpec(memory_space=pltpu.VMEM)
    gain, part, onehot = pl.pallas_call(
        functools.partial(prep_kernel, sizes),
        out_shape=[
            jax.ShapeDtypeStruct((channels, RADIX, 2 * RADIX), F32),
            jax.ShapeDtypeStruct((channels, 2 * RADIX, 2 * RADIX), F32),
            jax.ShapeDtypeStruct((LOW_BINS, samples), BF16),
        ],
        in_specs=[in_vmem] * (len(sizes) + 3),
        out_specs=[in_vmem] * 3,
        compiler_params=pltpu.CompilerParams(vmem_limit_bytes=24 * 2**20),
        cost_estimate=pl.CostEstimate(
            flops=4 * 10**9, bytes_accessed=9 * 2**20, transcendentals=0
        ),
        name="prep",
    )(*curs, chirp, bins, tables[1])
    constants = (tables[0], *tables[2:], twist)
    ready = []
    for chunk, size in enumerate(sizes[:-1]):
        ready.append(
            pl.pallas_call(
                functools.partial(filter_channels, sum(sizes[:chunk]), size),
                out_shape=jax.ShapeDtypeStruct((HALF * 4 * size, RADIX), F32),
                in_specs=[in_vmem] * 11,
                out_specs=in_vmem,
                compiler_params=pltpu.CompilerParams(vmem_limit_bytes=24 * 2**20),
                cost_estimate=pl.CostEstimate(
                    flops=size * 10**9, bytes_accessed=size * 2**20, transcendentals=0
                ),
                name="filter",
            )(prevs[chunk], gain, part, *constants)
        )
    factor = 1.0 / float(samples * devices // BINS)
    return pl.pallas_call(
        functools.partial(work_kernel, sizes, devices, factor),
        out_shape=jax.ShapeDtypeStruct((channels, 4, BINS // devices), F32),
        in_specs=[in_vmem] * (len(ready) + 13),
        out_specs=in_vmem,
        scratch_shapes=[
            pltpu.VMEM((HALF * 4 * sizes[-1], RADIX), F32),
            pltpu.VMEM((8 * rows, samples), BF16),
            pltpu.VMEM((2, devices // 2, 8, RADIX), F32),
            pltpu.VMEM((devices // 2, 8, RADIX), F32),
            pltpu.VMEM((devices // 2, 8, RADIX), F32),
            pltpu.VMEM((devices // 2, 8, RADIX), F32),
            pltpu.SemaphoreType.DMA((2,)),
            pltpu.SemaphoreType.DMA((devices // 2,)),
            pltpu.SemaphoreType.DMA((devices // 2,)),
        ],
        compiler_params=pltpu.CompilerParams(
            collective_id=0, has_side_effects=True, vmem_limit_bytes=32 * 2**20
        ),
        name="work",
    )(*ready, onehot, bins, prevs[-1], gain, part, *constants)


def solution(mesh):
    placed = (P("freq", None, "tm"), P("freq", None), P("tm"))
    return jax.shard_map(
        shards, mesh=mesh, in_specs=placed, out_specs=P("freq", None, "tm"), check_vma=False
    )
```

```python
import functools

import jax
import jax.numpy as jnp
import numpy as np
from jax import lax
from jax.experimental import pallas as pl
from jax.experimental.pallas import tpu as pltpu
from jax.sharding import PartitionSpec as P

BINS = 1024
RADIX = 128
HALF = 64
LOW_BINS = 256
F32 = jnp.float32
BF16 = jnp.bfloat16


def split_table(table):
    high = table.astype(jnp.bfloat16)
    low = (table - high.astype(np.float64)).astype(jnp.bfloat16)
    return high, low


def dft_tables():
    index = np.arange(RADIX)
    angle = 2.0 * np.pi * (index[:, None] * index[None, :] % RADIX) / RADIX
    four_real, four_imag = np.cos(angle), -np.sin(angle)
    turn = 2.0 * np.pi * (index[:, None] * index[None, :]) / (RADIX * RADIX)
    twist = np.concatenate([np.cos(turn), -np.sin(turn)], axis=1).astype(np.float32)
    left = np.block([[four_real, -four_imag], [four_imag, four_real]])
    right = np.block([[four_real, four_imag], [-four_imag, four_real]])
    back_right = np.block([[four_real, -four_imag], [four_imag, four_real]]) / RADIX
    kept_real, kept_imag = four_real[HALF:], four_imag[HALF:]
    back_left = np.block([[kept_real, kept_imag], [-kept_imag, kept_real]]) / RADIX
    tables = []
    for part in range(2):
        columns = np.arange(4 * HALF).reshape(4, HALF)[part::2].reshape(-1)
        tables.append(np.concatenate(split_table(left[:, columns]), axis=1))
    for table in (right, back_right, back_left):
        tables.extend(split_table(table))
    return tables, twist


def halves(value):
    high = value.astype(BF16)
    low = (value - high.astype(F32)).astype(BF16)
    return high, low


def dot(a, b):
    return jnp.dot(a, b, preferred_element_type=F32)


def cos_sin(phase):
    half = phase * 0.5
    square = half * half
    sine = half * (
        1.0 + square * (-1.0 / 6 + square * (1.0 / 120 + square * (-1.0 / 5040 + square * (
            1.0 / 362880 + square * (-1.0 / 39916800 + square * (1.0 / 6227020800))))))
    )
    cosine = 1.0 + square * (-1.0 / 2 + square * (1.0 / 24 + square * (-1.0 / 720 + square * (
        1.0 / 40320 + square * (-1.0 / 3628800 + square * (
            1.0 / 479001600 + square * (-1.0 / 87178291200))))))
    )
    return 1.0 - 2.0 * sine * sine, 2.0 * sine * cosine


def paired(block, base, part):
    return jnp.concatenate([block[base + part], block[base + 2 + part]], axis=1)


def first_stage(table, block, base):
    series = jnp.concatenate([paired(block, base, 0), paired(block, base, 1)], axis=0)
    return dot(table[...], jnp.concatenate([series, series], axis=0))


def prep_kernel(sizes, *refs):
    curs, (chirp, bins, left, gain, part, onehot) = refs[:len(sizes)], refs[len(sizes):]
    lane_bins = lax.broadcasted_iota(jnp.int32, (LOW_BINS, 2 * RADIX), 0)

    for chunk, cur in enumerate(curs):
        start = sum(sizes[:chunk])

        def channel(c, carry):
            cosine, sine = cos_sin(chirp[start + c].T)
            gain[start + c] = jnp.concatenate([cosine, sine], axis=1)
            part[start + c] = first_stage(left, cur, 4 * c)
            return carry

        lax.fori_loop(0, sizes[chunk], channel, 0)

    def mark(m, carry):
        own = bins[pl.ds(m, 1), :]
        columns = pl.ds(pl.multiple_of(m * 2 * RADIX, 2 * RADIX), 2 * RADIX)
        onehot[:, columns] = jnp.where(
            lane_bins == own - own // LOW_BINS * LOW_BINS, 1.0, 0.0
        ).astype(BF16)
        return carry

    lax.fori_loop(0, HALF // 2, mark, 0)


def filter_channels(
    start, size, prev, gain, part, left, right_h, right_l, back_right_h, back_right_l,
    back_left_h, back_left_l, twist, stokes,
):
    rows = 4 * size
    twist_real = twist[:, :RADIX]
    twist_imag = twist[:, RADIX:]
    wide_real = jnp.concatenate([twist_real, twist_real], axis=1)
    wide_imag = jnp.concatenate([twist_imag, twist_imag], axis=1)

    def channel(c):
        base = 4 * c
        section = part[start + c] + first_stage(left, prev, base)
        real, imag = section[:RADIX], section[RADIX:]
        turned_real = real * wide_real - imag * wide_imag
        turned_imag = real * wide_imag + imag * wide_real
        gain_real, gain_imag = gain[start + c, :, :RADIX], gain[start + c, :, RADIX:]
        waves_real, waves_imag = [], []
        for p in range(2):
            lanes = slice(p * RADIX, (p + 1) * RADIX)
            high, low = halves(
                jnp.concatenate([turned_real[:, lanes], turned_imag[:, lanes]], axis=1)
            )
            spec = dot(high, right_h[...]) + dot(low, right_h[...]) + dot(high, right_l[...])
            spec_real, spec_imag = spec[:, :RADIX], spec[:, RADIX:]
            high, low = halves(
                jnp.concatenate(
                    [
                        spec_real * gain_real - spec_imag * gain_imag,
                        spec_real * gain_imag + spec_imag * gain_real,
                    ],
                    axis=1,
                )
            )
            back = (
                dot(high, back_right_h[...])
                + dot(low, back_right_h[...])
                + dot(high, back_right_l[...])
            )
            back_real, back_imag = back[:, :RADIX], back[:, RADIX:]
            waves_real.append(back_real * twist_real + back_imag * twist_imag)
            waves_imag.append(back_imag * twist_real - back_real * twist_imag)
        high, low = halves(
            jnp.concatenate(
                [jnp.concatenate(waves_real, axis=1), jnp.concatenate(waves_imag, axis=1)], axis=0
            )
        )
        wave = (
            dot(back_left_h[...], high) + dot(back_left_h[...], low) + dot(back_left_l[...], high)
        )
        xr, xi = wave[:HALF, :RADIX], wave[HALF:, :RADIX]
        yr, yi = wave[:HALF, RADIX:], wave[HALF:, RADIX:]
        first = xr * xr + xi * xi
        second = yr * yr + yi * yi
        stokes[pl.ds(base, HALF, rows), :] = first + second
        stokes[pl.ds(base + 1, HALF, rows), :] = first - second
        stokes[pl.ds(base + 2, HALF, rows), :] = 2.0 * (xr * yr + xi * yi)
        stokes[pl.ds(base + 3, HALF, rows), :] = 2.0 * (xr * yi - xi * yr)

    def channel_pair(i, carry):
        channel(2 * i)
        channel(2 * i + 1)
        return carry

    lax.fori_loop(0, size // 2, channel_pair, 0)


def work_kernel(sizes, devices, factor, *refs):
    ready, refs = refs[:len(sizes) - 1], refs[len(sizes) - 1:]
    onehot, bins, *operands = refs[:13]
    out, last, picked, tiles, swapped, sums, landed, *sems = refs[13:]
    swap_sems, send_sems, recv_sems = sems
    me = lax.axis_index("tm")
    barrier = pltpu.get_barrier_semaphore()

    chips = devices // 2
    half = chips // 2
    core, chip = lax.rem(me, 2), me // 2
    side, place = chip // half, lax.rem(chip, half)
    partner = me + 1 - 2 * core

    def peer_chip(i):
        other = lax.rem(side + 1 - i // half, 2)
        return other * half + lax.rem(place + i, half)

    def greet(device):
        pl.semaphore_signal(
            barrier, inc=1, device_id={"tm": device}, device_id_type=pl.DeviceIdType.MESH
        )

    def greet_chip(i, carry):
        greet(peer_chip(i) * 2 + core)
        return carry

    steps = [(0, half), (half + 1, chips)]
    for low, high in steps:
        lax.fori_loop(low, high, greet_chip, 0)
    greet(partner)

    start = sum(sizes[:-1])
    filter_channels(start, sizes[-1], *operands, last)
    stokes = (*ready, last)
    rows = 4 * sum(sizes)
    groups = BINS // LOW_BINS

    def pick(m, carry):
        pieces = []
        for array, size in zip(stokes, sizes):
            count = 4 * size
            at = pl.multiple_of(m * 2 * count, 2 * count)
            pieces.append(
                jnp.concatenate(
                    [array[pl.ds(at, count), :], array[pl.ds(at + count, count), :]], axis=1
                )
            )
        value = jnp.concatenate(pieces, axis=0)
        high = value.astype(BF16).astype(F32)
        both = jnp.concatenate([high, value - high], axis=0)
        group = bins[pl.ds(m, 1), :] // LOW_BINS
        columns = pl.ds(pl.multiple_of(m * 2 * RADIX, 2 * RADIX), 2 * RADIX)
        for q in range(groups):
            picked[pl.ds(q * 2 * rows, 2 * rows), columns] = jnp.where(
                group == q, both, 0.0
            ).astype(BF16)
        return carry

    lax.fori_loop(0, HALF // 2, pick, 0, unroll=4)

    total = lax.dot_general(
        picked[...], onehot[...], (((1,), (1,)), ((), ())), preferred_element_type=F32
    )
    for q in range(groups):
        at = q * 2 * rows
        folded = total[at:at + rows] + total[at + rows:at + 2 * rows]
        for h in range(2):
            for b in range(4):
                lanes = slice(h * RADIX + 32 * b, h * RADIX + 32 * b + 32)
                tiles[b % 2, q * 4 + h * 2 + b // 2] = jnp.concatenate(
                    [folded[8 * a:8 * a + 8, lanes] for a in range(4)], axis=1
                )

    pl.semaphore_wait(barrier, chips)

    swap = pltpu.make_async_remote_copy(
        src_ref=tiles.at[1 - core],
        dst_ref=swapped,
        send_sem=swap_sems.at[0],
        recv_sem=swap_sems.at[1],
        device_id={"tm": partner},
        device_id_type=pl.DeviceIdType.MESH,
    )
    swap.start()
    swap.wait_recv()
    sums[...] = tiles[core] + swapped[...]

    def copy(i):
        peer = peer_chip(i)
        return pltpu.make_async_remote_copy(
            src_ref=sums.at[peer],
            dst_ref=landed.at[i],
            send_sem=send_sems.at[i],
            recv_sem=recv_sems.at[i],
            device_id={"tm": peer * 2 + core},
            device_id_type=pl.DeviceIdType.MESH,
        )

    def send(i, carry):
        copy(i).start()
        return carry

    def take(i, total):
        copy(i).wait_recv()
        return total + landed[i]

    for low, high in steps:
        lax.fori_loop(low, high, send, 0)
    total = sums[chip]
    for low, high in reversed(steps):
        total = lax.fori_loop(low, high, take, total)
    total = total * factor
    for a in range(4):
        for k in range(2):
            out[2 * a + k] = total[4 * k:4 * k + 4, 32 * a:32 * a + 32]

    swap.wait_send()

    def drain(i, carry):
        copy(i).wait_send()
        return carry

    for low, high in steps:
        lax.fori_loop(low, high, drain, 0)


def shards(baseband, chirp_phase, phase_bins):
    channels, _, samples = baseband.shape
    devices = lax.axis_size("tm")
    rows = 4 * channels
    sizes = (channels // 2, channels // 2)
    route = [(i, i + 1) for i in range(devices - 1)]
    curs, prevs = [], []
    for chunk, size in enumerate(sizes):
        start = sum(sizes[:chunk])
        cur = baseband[start:start + size].reshape(4 * size, HALF, RADIX)
        curs.append(cur)
        cur, baseband = lax.optimization_barrier((cur, baseband))
        prevs.append(lax.ppermute(cur, "tm", route))
    chirp = chirp_phase.reshape(channels, RADIX, RADIX)
    bins = phase_bins.reshape(samples // (2 * RADIX), 2 * RADIX)
    tables, twist = dft_tables()
    in_vmem = pl.BlockSpec(memory_space=pltpu.VMEM)
    gain, part, onehot = pl.pallas_call(
        functools.partial(prep_kernel, sizes),
        out_shape=[
            jax.ShapeDtypeStruct((channels, RADIX, 2 * RADIX), F32),
            jax.ShapeDtypeStruct((channels, 2 * RADIX, 2 * RADIX), F32),
            jax.ShapeDtypeStruct((LOW_BINS, samples), BF16),
        ],
        in_specs=[in_vmem] * (len(sizes) + 3),
        out_specs=[in_vmem] * 3,
        compiler_params=pltpu.CompilerParams(vmem_limit_bytes=24 * 2**20),
        cost_estimate=pl.CostEstimate(
            flops=4 * 10**9, bytes_accessed=9 * 2**20, transcendentals=0
        ),
        name="prep",
    )(*curs, chirp, bins, tables[1])
    constants = (tables[0], *tables[2:], twist)
    ready = []
    for chunk, size in enumerate(sizes[:-1]):
        ready.append(
            pl.pallas_call(
                functools.partial(filter_channels, sum(sizes[:chunk]), size),
                out_shape=jax.ShapeDtypeStruct((HALF * 4 * size, RADIX), F32),
                in_specs=[in_vmem] * 11,
                out_specs=in_vmem,
                compiler_params=pltpu.CompilerParams(vmem_limit_bytes=24 * 2**20),
                cost_estimate=pl.CostEstimate(
                    flops=size * 10**9, bytes_accessed=size * 2**20, transcendentals=0
                ),
                name="filter",
            )(prevs[chunk], gain, part, *constants)
        )
    factor = 1.0 / float(samples * devices // BINS)
    return pl.pallas_call(
        functools.partial(work_kernel, sizes, devices, factor),
        out_shape=jax.ShapeDtypeStruct((channels, 4, BINS // devices), F32),
        in_specs=[in_vmem] * (len(ready) + 13),
        out_specs=in_vmem,
        scratch_shapes=[
            pltpu.VMEM((HALF * 4 * sizes[-1], RADIX), F32),
            pltpu.VMEM((8 * rows, samples), BF16),
            pltpu.VMEM((2, devices // 2, 8, RADIX), F32),
            pltpu.VMEM((devices // 2, 8, RADIX), F32),
            pltpu.VMEM((devices // 2, 8, RADIX), F32),
            pltpu.VMEM((devices // 2, 8, RADIX), F32),
            pltpu.SemaphoreType.DMA((2,)),
            pltpu.SemaphoreType.DMA((devices // 2,)),
            pltpu.SemaphoreType.DMA((devices // 2,)),
        ],
        compiler_params=pltpu.CompilerParams(
            collective_id=0, has_side_effects=True, vmem_limit_bytes=32 * 2**20
        ),
        name="work",
    )(*ready, onehot, bins, prevs[-1], gain, part, *constants)


def solution(mesh):
    placed = (P("freq", None, "tm"), P("freq", None), P("tm"))
    return jax.shard_map(
        shards, mesh=mesh, in_specs=placed, out_specs=P("freq", None, "tm"), check_vma=False
    )
```
